512 devices in a mesh: grp: 16 (over x, y), dev: 32 (over z, core).
Axes of the slice: x: 4, y: 4, z: 16, core: 2. Of those that a mesh axis runs over, the one named last changes fastest.
Arguments:
- rhs: float32 [16, 524288], P(None, ('grp', 'dev')), may hold values from -6 to 6
- leaf_basis: float32 [64, 524288], P(None, ('grp', 'dev'))
- near_blocks: float32 [64, 1048576], P(None, ('grp', 'dev')), may hold values from -0.75 to 0.75
- near_partner: int32 [8192], P(('grp', 'dev')), may hold values from 0 to 8191, as said below
- local_transfer: float32 [64, 983040], P(None, ('grp', 'dev'))
- local_coupling: float32 [64, 983040], P(None, ('grp', 'dev')), may hold values from -0.75 to 0.75
- far_partner: int32 [512, 30], P(('grp', 'dev')), may hold values from 0 to 8191, as said below
- dev_transfer: float32 [16, 64, 3968], P('grp')
- dev_coupling: float32 [16, 64, 3968], P('grp'), may hold values from -4 to 4
- grp_transfer: float32 [64, 1920], replicated
- grp_coupling: float32 [64, 1920], replicated, may hold values from -6 to 6
Outputs:
- product: float32 [16, 524288], P(None, ('grp', 'dev'))
- root_factor: float32 [64, 64], replicated
The draws below stay inside these ranges and needn't reach their ends.
Inputs may be any that keep to these rules, and one draw needn't show every extreme that they name: near_partner[l] is a leaf other than l, at most 16 leaves away; some leaf's partner is exactly 16 leaves away. `far_partner`: in row s, entry 2 * 16 - 2 * m + j (m = 16 >> k, level k, 0 <= j < m) names a node of level k other than node s * m + j and at most m nodes from it; at every level some entry is exactly m nodes away.
All inputs are finite; a program needn't handle non-finite values.
Results may differ from the reference program's by a relative error of at most 0.0001.
Values sent between devices are 32-bit elements; how exact they have to be, the bound alone decides.
A program may use at most 64 MiB of HBM per device.

```python
import math
import jax
import jax.numpy as jnp
from jax import lax

RANK = 64
LEAF = 64
NRHS = 16
LOC = 4
LEAF_DEV = 16
LOG_DEV = 5
LOG_GRP = 4
GROUPS = 16
SUBTREES = 512
LEAVES = 8192
UNKNOWNS = 524288
LOCAL_NODES = 30
DEV_NODES = 62
GRP_NODES = 30
N_GRP = 16
N_DEV = 32


def spread_partner(key, node_count, reach_nodes):
    first_key, second_key, third_key = jax.random.split(key, 3)
    distance = jax.random.randint(first_key, (node_count,), 1, reach_nodes + 1)
    longest = jax.random.randint(second_key, (), 0, node_count)
    node_ids = jnp.arange(node_count)
    distance = jnp.where(node_ids == longest, reach_nodes, distance)
    direction = 2 * jax.random.randint(third_key, (node_count,), 0, 2) - 1
    forward = node_ids + direction * distance
    backward = node_ids - direction * distance
    inside = (forward >= 0) & (forward < node_count)
    return jnp.where(inside, forward, backward).astype(jnp.int32)


def near_identity(key, leading, row_count, block_width, block_count, scale):
    array_shape = leading + (row_count, block_count * block_width)
    noise_part = jax.random.normal(key, array_shape, jnp.float32)
    diagonal = (jnp.arange(row_count)[:, None] == jnp.arange(block_count * block_width)[None, :] % block_width).astype(jnp.float32)
    return scale * (diagonal + 0.35 / math.sqrt(block_width) * noise_part)


def draw_leaf_basis(key, part):
    basis = near_identity(jax.random.fold_in(key, 3), (), LEAF, RANK, LEAVES, 1.0)
    return basis


def draw_near_partner(key, part):
    return spread_partner(jax.random.fold_in(key, 11), LEAVES, LEAF_DEV)


def draw_far_partner(key, part):
    columns = []
    for tree_level in range(LOC):
        level_nodes = LEAF_DEV >> tree_level
        chosen = spread_partner(jax.random.fold_in(key, 100 + tree_level), SUBTREES * level_nodes, level_nodes)
        columns.append(chosen.reshape(SUBTREES, level_nodes))
    return jnp.concatenate(columns, axis=1)


def draw_local_transfer(key, part):
    return near_identity(jax.random.fold_in(key, 21), (), RANK, RANK, SUBTREES * LOCAL_NODES, 0.70710678)


def draw_dev_transfer(key, part):
    return near_identity(jax.random.fold_in(key, 31), (GROUPS,), RANK, RANK, DEV_NODES, 0.70710678)


def draw_grp_transfer(key, part):
    return near_identity(jax.random.fold_in(key, 41), (), RANK, RANK, GRP_NODES, 0.70710678)


def block_levels(stream_key, dims, shards, smallest, largest):
    def one(axis_at, parts):
        draws = jax.random.uniform(jax.random.fold_in(jax.random.fold_in(stream_key, 6), axis_at), (parts,), jnp.float32, smallest / len(shards), largest / len(shards))
        return jnp.repeat(jnp.exp(draws), dims[axis_at] // parts).reshape((-1,) + (1,) * (len(dims) - axis_at - 1))

    loudness = one(*shards[0])
    for cut in shards[1:]:
        loudness = loudness * one(*cut)
    return loudness


def gaussian(stream_key, shape, width, limit, cuts=(), kind=jnp.bfloat16):
    array = jax.random.normal(stream_key, shape, jnp.float32) * width
    if len(cuts) > 0:
        array = block_levels(stream_key, shape, cuts, -0.22, 0.18) * array
    return jnp.clip(array, min=-limit, max=limit).astype(kind)


def setup_inputs(seed: int = 0) -> dict:
    seeds = jax.random.split(jax.random.key(seed), 12)
    return {
        "rhs": gaussian(seeds[0], (NRHS, UNKNOWNS), 1.0, 6.0, ((1, 512),), jnp.float32),
        "leaf_basis": draw_leaf_basis(jax.random.fold_in(seeds[11], 71), 0),
        "near_blocks": gaussian(seeds[2], (LEAF, 2 * LEAVES * LEAF), LEAF ** -0.5, 0.75, ((1, 512),), jnp.float32),
        "near_partner": draw_near_partner(jax.random.fold_in(seeds[11], 71), 0),
        "local_transfer": draw_local_transfer(jax.random.fold_in(seeds[11], 71), 0),
        "local_coupling": gaussian(seeds[5], (RANK, SUBTREES * LOCAL_NODES * RANK), RANK ** -0.5, 0.75, ((1, 512),), jnp.float32),
        "far_partner": draw_far_partner(jax.random.fold_in(seeds[11], 71), 0),
        "dev_transfer": draw_dev_transfer(jax.random.fold_in(seeds[11], 71), 0),
        "dev_coupling": gaussian(seeds[8], (GROUPS, RANK, DEV_NODES * RANK), (2.0 / RANK ** 0.5), 4.0, ((0, 16),), jnp.float32),
        "grp_transfer": draw_grp_transfer(jax.random.fold_in(seeds[11], 71), 0),
        "grp_coupling": gaussian(seeds[10], (RANK, GRP_NODES * RANK), (6.0 / RANK ** 0.5), 6.0, (), jnp.float32),
    }


precise = lax.Precision.HIGHEST

def blocks_of(matrix, node_count):
    return matrix.reshape(matrix.shape[0], node_count, -1).transpose(1, 0, 2)

def lower_solve(factor, right_side, transpose):
    return jax.scipy.linalg.solve_triangular(factor, right_side, trans=transpose, lower=True)

def combine(factors, projected, transfers):
    upper_blocks = jnp.einsum('nji,njk->nik', factors, transfers, precision=precise)
    even_upper = upper_blocks[0::2]
    odd_upper = upper_blocks[1::2]
    gram_matrix = jnp.einsum('nji,njk->nik', even_upper, even_upper, precision=precise) + jnp.einsum('nji,njk->nik', odd_upper, odd_upper, precision=precise)
    parent = jnp.linalg.cholesky(gram_matrix)
    summed = jnp.einsum('nji,njr->nir', even_upper, projected[0::2], precision=precise) + jnp.einsum('nji,njr->nir', odd_upper, projected[1::2], precision=precise)
    return (upper_blocks, parent, lower_solve(parent, summed, 0))

def sibling(stacked):
    return stacked.reshape((-1, 2) + stacked.shape[1:])[:, ::-1].reshape(stacked.shape)

def reference(rhs, leaf_basis, near_blocks, near_partner, local_transfer, local_coupling, far_partner, dev_transfer, dev_coupling, grp_transfer, grp_coupling):
    leaf_bases = leaf_basis.reshape(LEAF, LEAVES, RANK).transpose(1, 0, 2)
    points = rhs.reshape(NRHS, LEAVES, LEAF)
    factors = jnp.linalg.cholesky(jnp.einsum('lpi,lpk->lik', leaf_bases, leaf_bases, precision=precise))
    projected = lower_solve(factors, jnp.einsum('lpk,rlp->lkr', leaf_bases, points, precision=precise), 0)
    local_trans = local_transfer.reshape(RANK, SUBTREES, LOCAL_NODES, RANK).transpose(1, 2, 0, 3)
    local_couple = local_coupling.reshape(RANK, SUBTREES, LOCAL_NODES, RANK).transpose(1, 2, 0, 3)
    dev_trans = dev_transfer.reshape(GROUPS, RANK, DEV_NODES, RANK).transpose(0, 2, 1, 3)
    dev_couple = dev_coupling.reshape(GROUPS, RANK, DEV_NODES, RANK).transpose(0, 2, 1, 3)
    grp_trans = blocks_of(grp_transfer, GRP_NODES)
    grp_couple = blocks_of(grp_coupling, GRP_NODES)
    level_factors = [factors]
    level_upper = []
    level_coupled = []
    offset = 0
    for tree_level in range(LOC):
        level_nodes = LEAF_DEV >> tree_level
        transfers = local_trans[:, offset:offset + level_nodes].reshape(-1, RANK, RANK)
        couplings = local_couple[:, offset:offset + level_nodes].reshape(-1, RANK, RANK)
        partners = far_partner[:, offset:offset + level_nodes].reshape(-1)
        level_coupled.append(jnp.einsum('nik,nkr->nir', couplings, projected[partners], precision=precise))
        upper_blocks, factors, projected = combine(factors, projected, transfers)
        level_upper.append(upper_blocks)
        level_factors.append(factors)
        offset += level_nodes
    offset = 0
    for tree_level in range(LOG_DEV):
        level_nodes = N_DEV >> tree_level
        transfers = dev_trans[:, offset:offset + level_nodes].reshape(-1, RANK, RANK)
        couplings = dev_couple[:, offset:offset + level_nodes].reshape(-1, RANK, RANK)
        level_coupled.append(jnp.einsum('nik,nkr->nir', couplings, sibling(projected), precision=precise))
        upper_blocks, factors, projected = combine(factors, projected, transfers)
        level_upper.append(upper_blocks)
        level_factors.append(factors)
        offset += level_nodes
    offset = 0
    for tree_level in range(LOG_GRP):
        level_nodes = N_GRP >> tree_level
        transfers = grp_trans[offset:offset + level_nodes]
        couplings = grp_couple[offset:offset + level_nodes]
        level_coupled.append(jnp.einsum('nik,nkr->nir', couplings, sibling(projected), precision=precise))
        upper_blocks, factors, projected = combine(factors, projected, transfers)
        level_upper.append(upper_blocks)
        level_factors.append(factors)
        offset += level_nodes
    root_factor = factors[0]
    downward = jnp.zeros((1, RANK, NRHS), jnp.float32)
    for tree_level in reversed(range(len(level_upper))):
        lifted = lower_solve(level_factors[tree_level + 1], downward, 1)
        downward = level_coupled[tree_level] + jnp.einsum('nik,nkr->nir', level_upper[tree_level], jnp.repeat(lifted, 2, axis=0), precision=precise)
    lifted = lower_solve(level_factors[0], downward, 1)
    far_part = jnp.einsum('lpk,lkr->rlp', leaf_bases, lifted, precision=precise)
    near_grid = near_blocks.reshape(LEAF, LEAVES, 2, LEAF)
    near_part = jnp.einsum('plq,rlq->rlp', near_grid[:, :, 0], points, precision=precise) + jnp.einsum('plq,rlq->rlp', near_grid[:, :, 1], points[:, near_partner], precision=precise)
    product = (near_part + far_part).reshape(NRHS, UNKNOWNS)
    return (product, root_factor)
```

```python
import jax
import jax.numpy as jnp
from jax import lax
from jax.experimental import pallas as pl
from jax.experimental.pallas import tpu as pltpu
from jax.sharding import PartitionSpec as P

RANK = 64
NRHS = 16
LOC_PAIRS = 15
PAIR_BASE = (0, 8, 12, 14)
LOG_DEV = 5
LOG_GRP = 4
UP = LOG_DEV + LOG_GRP
BLOCK = 16
CHUNK = 5
MESH = pl.DeviceIdType.MESH
f32 = jnp.float32


def dot(a, b, ca, cb):
    return lax.dot_general(
        a,
        b,
        (((ca,), (cb,)), ((), ())),
        precision=lax.Precision.HIGHEST,
        preferred_element_type=f32,
    )


def nn(a, b):
    return dot(a, b, 1, 0)


def nt(a, b):
    return dot(a, b, 1, 1)


def tn(a, b):
    return dot(a, b, 0, 0)


def left_of(rows):
    return lax.broadcasted_iota(jnp.int32, (rows, 128), 1) < 64


def swap(p):
    return pltpu.roll(p, 64, 1)


def fold(p):
    return p + swap(p)


def pick(a, b):
    return jnp.where(left_of(a.shape[0]), a, b)


def bd(p):
    left = left_of(64)
    return jnp.concatenate([jnp.where(left, p, 0.0), jnp.where(left, 0.0, p)], axis=0)


def diag(c):
    return pick(c[:64], c[64:])


def dups(p):
    s = swap(p)
    return pick(p, s), pick(s, p)


def merge(g, z, e):
    be = bd(e)
    return fold(diag(tn(be, nn(bd(g), be)))), fold(nn(z, be))


def factor_chunk(load, store, scratch, pairs):
    row = lax.broadcasted_iota(jnp.int32, (64, 128), 0)
    lane = lax.broadcasted_iota(jnp.int32, (64, 128), 1)
    left = lane < 64
    eye_left = jnp.where(row == lane, 1.0, 0.0)
    eye_right = jnp.where(row == lane - 64, 1.0, 0.0)
    for p in range(pairs):
        s = swap(load(p))
        scratch[2 * p] = jnp.where(left, eye_left, s)
        scratch[2 * p + 1] = jnp.where(left, s, eye_right)
    nodes = 2 * pairs
    rows = lax.broadcasted_iota(jnp.int32, (BLOCK, 128), 0)
    for k in range(64 // BLOCK):
        lo = k * BLOCK
        cur = [scratch[n, lo : lo + BLOCK, :] for n in range(nodes)]
        piv = [jnp.ones((BLOCK, 128), f32)] * nodes
        for j in range(BLOCK):
            below = rows > j
            here = rows == j
            for n in range(nodes):
                c = lo + j + (64 if n % 2 == 0 else 0)
                r = cur[n]
                col = jnp.broadcast_to(r[:, c : c + 1], (BLOCK, 128))
                d = jnp.broadcast_to(col[j : j + 1, :], (BLOCK, 128))
                top = jnp.broadcast_to(r[j : j + 1, :], (BLOCK, 128))
                piv[n] = jnp.where(here, d, piv[n])
                if j < BLOCK - 1:
                    cur[n] = r - jnp.where(below, col, 0.0) * (top / d)
        for n in range(nodes):
            done = cur[n] * lax.rsqrt(piv[n])
            scratch[n, lo : lo + BLOCK, :] = done
            if lo + BLOCK < 64:
                half = 64 if n % 2 == 0 else 0
                left_rows = done.T[half + lo + BLOCK : half + 64, :]
                scratch[n, lo + BLOCK : 64, :] -= nn(left_rows, done)
    for p in range(pairs):
        store(p, jnp.where(left, scratch[2 * p], scratch[2 * p + 1]))


def factor_all(grams, inverses, scratch, count):
    @pl.loop(0, count // CHUNK)
    def _(i):
        def load(p):
            return grams[i * CHUNK + p]

        def store(p, value):
            inverses[i * CHUNK + p] = value

        factor_chunk(load, store, scratch, CHUNK)


def lanes(i):
    return slice(128 * i, 128 * i + 128)


def up_local(leaf, rhs, trans, grams, zs):
    for j in range(8):
        u = leaf[:, lanes(j)]
        grams[j] = diag(tn(u, u))
        zs[j] = nn(rhs[:, lanes(j)], bd(u))
    for k in range(4):
        base = PAIR_BASE[k]
        held = None
        for i in range(8 >> k):
            g, z = merge(grams[base + i], zs[base + i], trans[:, lanes(base + i)])
            if k == 3:
                return g, z
            if i % 2 == 0:
                held = (g, z)
            else:
                grams[PAIR_BASE[k + 1] + i // 2] = pick(held[0], g)
                zs[PAIR_BASE[k + 1] + i // 2] = pick(held[1], z)


def pack(g, z):
    return pick(g[:32], g[32:]), pick(z[:8], z[8:])


def unpack(pg, pz):
    g0, g1 = dups(pg)
    z0, z1 = dups(pz)
    return jnp.concatenate([g0, g1], 0), jnp.concatenate([z0, z1], 0)


def kernel_a(leaf, rhs, trans, inv, xhat, top, grams, zs, scratch):
    g, z = up_local(leaf, rhs, trans, grams, zs)
    pg, pz = pack(g, z)
    top[0:32, :] = pg
    top[32:40, :] = pz
    factor_all(grams, inv, scratch, LOC_PAIRS)
    for i in range(LOC_PAIRS):
        xhat[i] = nt(zs[i], bd(inv[i]))


def kernel_b(
    rhs,
    xhat,
    top,
    dev_trans,
    grp_trans,
    up_g,
    up_z,
    root_g,
    rhs_lo,
    rhs_hi,
    xhat_lo,
    xhat_hi,
    outgoing,
    incoming,
    send_sem,
    recv_sem,
    halo_send,
    halo_recv,
):
    grp = lax.axis_index("grp")
    dev = lax.axis_index("dev")
    place = grp * 32 + dev
    after = lax.rem(place + 1, 512)
    before = lax.rem(place + 511, 512)
    right = (after // 32, lax.rem(after, 32))
    left = (before // 32, lax.rem(before, 32))
    peers = []
    for b in range(UP):
        if b < LOG_DEV:
            bit = lax.rem(dev // (1 << b), 2)
            peers.append((grp, dev + (1 - 2 * bit) * (1 << b)))
        else:
            w = 1 << (b - LOG_DEV)
            bit = lax.rem(grp // w, 2)
            peers.append((grp + (1 - 2 * bit) * w, dev))
    barrier = pltpu.get_barrier_semaphore()
    for peer in peers + [left, right]:
        pl.semaphore_signal(barrier, inc=1, device_id=peer, device_id_type=MESH)
    pl.semaphore_wait(barrier, UP + 2)

    def copy(src, dst, s, r, peer):
        return pltpu.make_async_remote_copy(
            src_ref=src,
            dst_ref=dst,
            send_sem=s,
            recv_sem=r,
            device_id=peer,
            device_id_type=MESH,
        )

    halos = [
        copy(rhs, rhs_lo, halo_send.at[0], halo_recv.at[0], right),
        copy(rhs, rhs_hi, halo_send.at[1], halo_recv.at[1], left),
        copy(xhat, xhat_lo, halo_send.at[2], halo_recv.at[2], right),
        copy(xhat, xhat_hi, halo_send.at[3], halo_recv.at[3], left),
    ]
    outgoing[0] = top[...]
    own_g, own_z = unpack(top[0:32, :], top[32:40, :])
    half = lax.broadcasted_iota(jnp.int32, (64, 128), 1) // 64
    for b in range(UP):
        step = copy(
            outgoing.at[b], incoming.at[b], send_sem.at[b], recv_sem.at[b], peers[b]
        )
        step.start()
        if b < 4:
            halos[b].start()
        pos = dev if b < LOG_DEV else grp
        lev = b if b < LOG_DEV else b - LOG_DEV
        size = 32 if b < LOG_DEV else 16
        bit = lax.rem(pos // (1 << lev), 2)
        pair = size - (size >> lev) + pos // (2 << lev)
        at = pl.ds(pl.multiple_of(pair * 128, 128), 128)
        e = dev_trans[0, :, at] if b < LOG_DEV else grp_trans[:, at]
        mine = half == bit
        step.wait()
        sib_g, sib_z = unpack(incoming[b, 0:32, :], incoming[b, 32:40, :])
        g = jnp.where(mine, own_g, sib_g)
        z = jnp.where(mine[:16], own_z, sib_z)
        up_g[b] = g
        up_z[b] = z
        own_g, own_z = merge(g, z, e)
        if b + 1 < UP:
            pg, pz = pack(own_g, own_z)
            outgoing[b + 1, 0:32, :] = pg
            outgoing[b + 1, 32:40, :] = pz
    root_g[...] = own_g
    for halo in halos:
        halo.wait()


def kernel_c(
    info,
    near_at,
    far_at,
    leaf,
    rhs,
    rhs_lo,
    rhs_hi,
    near,
    trans,
    couple,
    inv,
    xhat,
    xhat_lo,
    xhat_hi,
    up_g,
    up_z,
    root_g,
    dev_trans,
    dev_couple,
    grp_trans,
    grp_couple,
    product,
    root,
    grams,
    up_inv,
    scratch,
    points,
    nodes,
):
    half = lax.broadcasted_iota(jnp.int32, (16, 128), 1) // 64
    for i in range(UP):
        grams[i] = up_g[i]
    grams[UP] = root_g[...]
    factor_all(grams, up_inv, scratch, UP + 1)
    last = scratch[2 * CHUNK - 1]
    upper = lax.broadcasted_iota(jnp.int32, (64, 128), 0) <= lax.broadcasted_iota(
        jnp.int32, (64, 128), 1
    )
    root[...] = jnp.where(upper, last, 0.0)[:, :64].T

    for s, block in enumerate((rhs_lo, rhs, rhs_hi)):
        for j in range(8):
            a, b = dups(block[:, lanes(j)])
            points[16 * s + 2 * j] = a
            points[16 * s + 2 * j + 1] = b
    for k in range(4):
        size = 16 >> k
        for s, block in enumerate((xhat_lo, xhat, xhat_hi)):
            for j in range(size // 2):
                a, b = dups(block[PAIR_BASE[k] + j])
                at = 6 * PAIR_BASE[k] + size * s + 2 * j
                nodes[at] = a
                nodes[at + 1] = b

    v = None
    for b in reversed(range(UP)):
        pos = info[1] if b < LOG_DEV else info[0]
        lev = b if b < LOG_DEV else b - LOG_DEV
        size = 32 if b < LOG_DEV else 16
        bit = lax.rem(pos // (1 << lev), 2)
        pair = size - (size >> lev) + pos // (2 << lev)
        at = pl.ds(pl.multiple_of(pair * 128, 128), 128)
        e = dev_trans[0, :, at] if b < LOG_DEV else grp_trans[:, at]
        c = dev_couple[0, :, at] if b < LOG_DEV else grp_couple[:, at]
        bi = bd(up_inv[b])
        t = nn(nt(swap(nt(up_z[b], bi)), bd(c)), bi)
        if v is not None:
            t = t + nt(v, bd(e))
        v = jnp.where(half == bit, t, swap(t))

    held = [v]
    for k in reversed(range(4)):
        base = PAIR_BASE[k]
        grown = []
        for i in range(8 >> k):
            p = base + i
            qa = 6 * base + far_at[2 * p]
            qb = 6 * base + far_at[2 * p + 1]
            x = pick(nodes[qa], nodes[qb])
            y = nt(x, bd(couple[:, lanes(p)]))
            t = nn(y, bd(inv[p])) + nt(held[i], bd(trans[:, lanes(p)]))
            if k > 0:
                grown.extend(dups(t))
            else:
                far = nt(t, bd(leaf[:, lanes(i)]))
                cat = jnp.concatenate(
                    [
                        pick(points[16 + 2 * i], points[near_at[2 * i]]),
                        pick(points[17 + 2 * i], points[near_at[2 * i + 1]]),
                    ],
                    0,
                )
                d = jnp.concatenate([near[:, lanes(2 * i)], near[:, lanes(2 * i + 1)]], 0)
                o = nt(cat, d)
                product[:, lanes(i)] = pick(o[:16], o[16:]) + far
        held = grown


def shards(
    rhs,
    leaf_basis,
    near_blocks,
    near_partner,
    local_transfer,
    local_coupling,
    far_partner,
    dev_transfer,
    dev_coupling,
    grp_transfer,
    grp_coupling,
):
    dev = lax.axis_index("dev")
    grp = lax.axis_index("grp")
    place = grp * lax.axis_size("dev") + dev
    vmem = pl.BlockSpec(memory_space=pltpu.VMEM)
    smem = pl.BlockSpec(memory_space=pltpu.SMEM)

    def shape(*dims):
        return jax.ShapeDtypeStruct(dims, f32)

    inv, xhat, top = pl.pallas_call(
        kernel_a,
        name="local_up",
        out_shape=(shape(15, 64, 128), shape(15, 16, 128), shape(40, 128)),
        in_specs=[vmem] * 3,
        out_specs=(vmem,) * 3,
        scratch_shapes=[
            pltpu.VMEM((15, 64, 128), f32),
            pltpu.VMEM((15, 16, 128), f32),
            pltpu.VMEM((2 * CHUNK, 64, 128), f32),
        ],
    )(leaf_basis, rhs, local_transfer)

    up_g, up_z, root_g, rhs_lo, rhs_hi, xhat_lo, xhat_hi = pl.pallas_call(
        kernel_b,
        name="climb",
        out_shape=(
            shape(UP, 64, 128),
            shape(UP, 16, 128),
            shape(64, 128),
            shape(16, 1024),
            shape(16, 1024),
            shape(15, 16, 128),
            shape(15, 16, 128),
        ),
        in_specs=[vmem] * 5,
        out_specs=(vmem,) * 7,
        scratch_shapes=[
            pltpu.VMEM((UP, 40, 128), f32),
            pltpu.VMEM((UP, 40, 128), f32),
            pltpu.SemaphoreType.DMA((UP,)),
            pltpu.SemaphoreType.DMA((UP,)),
            pltpu.SemaphoreType.DMA((4,)),
            pltpu.SemaphoreType.DMA((4,)),
        ],
        compiler_params=pltpu.CompilerParams(collective_id=0, has_side_effects=True),
    )(rhs, xhat, top, dev_transfer, grp_transfer)

    sizes = jnp.repeat(jnp.array([16, 8, 4, 2], jnp.int32), jnp.array([16, 8, 4, 2]), total_repeat_length=30)
    info = jnp.stack([grp, dev]).astype(jnp.int32)
    near_at = near_partner - (place - 1) * 16
    far_at = far_partner[0] - (place - 1) * sizes

    return pl.pallas_call(
        kernel_c,
        name="down",
        out_shape=(shape(16, 1024), shape(64, 64)),
        in_specs=[smem] * 3 + [vmem] * 18,
        out_specs=(vmem,) * 2,
        scratch_shapes=[
            pltpu.VMEM((UP + 1, 64, 128), f32),
            pltpu.VMEM((UP + 1, 64, 128), f32),
            pltpu.VMEM((2 * CHUNK, 64, 128), f32),
            pltpu.VMEM((48, 16, 128), f32),
            pltpu.VMEM((90, 16, 128), f32),
        ],
    )(
        info,
        near_at,
        far_at,
        leaf_basis,
        rhs,
        rhs_lo,
        rhs_hi,
        near_blocks,
        local_transfer,
        local_coupling,
        inv,
        xhat,
        xhat_lo,
        xhat_hi,
        up_g,
        up_z,
        root_g,
        dev_transfer,
        dev_coupling,
        grp_transfer,
        grp_coupling,
    )


def solution(mesh):
    return jax.shard_map(
        shards,
        mesh=mesh,
        in_specs=(
            P(None, ("grp", "dev")),
            P(None, ("grp", "dev")),
            P(None, ("grp", "dev")),
            P(("grp", "dev")),
            P(None, ("grp", "dev")),
            P(None, ("grp", "dev")),
            P(("grp", "dev"), None),
            P("grp", None, None),
            P("grp", None, None),
            P(),
            P(),
        ),
        out_specs=(P(None, ("grp", "dev")), P()),
        check_vma=False,
    )
```

```python
import jax
import jax.numpy as jnp
from jax import lax
from jax.experimental import pallas as pl
from jax.experimental.pallas import tpu as pltpu
from jax.sharding import PartitionSpec as P

RANK = 64
NRHS = 16
LOC_PAIRS = 15
PAIR_BASE = (0, 8, 12, 14)
LOG_DEV = 5
LOG_GRP = 4
UP = LOG_DEV + LOG_GRP
FILL = 4
MESH = pl.DeviceIdType.MESH
f32 = jnp.float32
bf16 = jnp.bfloat16


def split(x):
    hi = x.astype(bf16)
    return hi, (x - hi.astype(f32)).astype(bf16)


def mm(a, b, ca, cb):
    return lax.dot_general(
        jnp.concatenate([a[0], a[1], a[0]], axis=ca),
        jnp.concatenate([b[0], b[0], b[1]], axis=cb),
        (((ca,), (cb,)), ((), ())),
        preferred_element_type=f32,
    )


def nn(a, b):
    return mm(a, b, 1, 0)


def nt(a, b):
    return mm(a, b, 1, 1)


def tn(a, b):
    return mm(a, b, 0, 0)


def left_of(rows):
    return lax.broadcasted_iota(jnp.int32, (rows, 128), 1) < 64


def swap(p):
    return pltpu.roll(p, 64, 1)


def fold(p):
    return p + swap(p)


def pick(a, b):
    return jnp.where(left_of(a.shape[0]), a, b)


def bd(pair):
    keep = left_of(64).astype(f32)
    left = keep.astype(bf16)
    right = (1.0 - keep).astype(bf16)
    return tuple(jnp.concatenate([x * left, x * right], axis=0) for x in pair)


def diag(c):
    return pick(c[:64], c[64:])


def dups(p):
    s = swap(p)
    return pick(p, s), pick(s, p)


def merge(g, z, e):
    es = split(e)
    lhs = tuple(jnp.concatenate([a, b], axis=0) for a, b in zip(bd(split(g)), split(z)))
    both = nn(lhs, bd(es))
    return fold(diag(tn(es, split(diag(both[:128]))))), fold(both[128:])


def factor(grams, inverses, scratch, pairs):
    row = lax.broadcasted_iota(jnp.int32, (64, 128), 0)
    lane = lax.broadcasted_iota(jnp.int32, (64, 128), 1)
    left = lane < 64
    eye_left = jnp.where(row == lane, 1.0, 0.0)
    eye_right = jnp.where(row == lane - 64, 1.0, 0.0)
    for p in range(pairs):
        s = swap(grams[p])
        scratch[2 * p] = jnp.where(left, eye_left, s)
        scratch[2 * p + 1] = jnp.where(left, s, eye_right)
    nodes = 2 * pairs
    rows = row[:8]
    for lo in range(0, 64, 16):
        cur = [[scratch[n, lo + h : lo + h + 8, :] for h in (0, 8)] for n in range(nodes)]
        for j in range(16):
            h, js = j // 8, j % 8
            here = rows == js
            below = rows > js
            for n in range(nodes):
                c = lo + j + (64 if n % 2 == 0 else 0)
                r = cur[n][h]
                col = jnp.broadcast_to(r[:, c : c + 1], (8, 128))
                inv = lax.rsqrt(jnp.broadcast_to(col[js : js + 1, :], (8, 128)))
                top = jnp.broadcast_to(r[js : js + 1, :], (8, 128)) * inv
                step = top * inv
                if js < 7:
                    r = r - jnp.where(below, col, 0.0) * step
                cur[n][h] = jnp.where(here, top, r)
                if h == 0:
                    r = cur[n][1]
                    cur[n][1] = r - jnp.broadcast_to(r[:, c : c + 1], (8, 128)) * step
        for n in range(nodes):
            done = jnp.concatenate(cur[n], axis=0)
            scratch[n, lo : lo + 16, :] = done
            if lo + 16 < 64:
                half = 64 if n % 2 == 0 else 0
                hi = done.astype(bf16).astype(f32)
                low = (done - hi).astype(bf16).astype(f32)
                across = jnp.concatenate([hi, low, hi], axis=0).T
                scratch[n, lo + 16 : 64, :] -= lax.dot_general(
                    across[half + lo + 16 : half + 64, :].astype(bf16),
                    jnp.concatenate([hi, hi, low], axis=0).astype(bf16),
                    (((1,), (0,)), ((), ())),
                    preferred_element_type=f32,
                )
    for p in range(pairs):
        inverses[p] = jnp.where(left, scratch[2 * p], scratch[2 * p + 1])


def lanes(i):
    return slice(128 * i, 128 * i + 128)


def up_leaves(leaf, rhs, grams, zs):
    for j in range(8):
        u = split(leaf[:, lanes(j)])
        grams[j] = diag(tn(u, u))
        zs[j] = nn(split(rhs[:, lanes(j)]), bd(u))


def up_local(trans, grams, zs):
    for k in range(4):
        base = PAIR_BASE[k]
        held = None
        for i in range(8 >> k):
            g, z = merge(grams[base + i], zs[base + i], trans[:, lanes(base + i)])
            if k == 3:
                return g, z
            if i % 2 == 0:
                held = (g, z)
            else:
                grams[PAIR_BASE[k + 1] + i // 2] = pick(held[0], g)
                zs[PAIR_BASE[k + 1] + i // 2] = pick(held[1], z)


def pack(g, z):
    return pick(g[:32], g[32:]), pick(z[:8], z[8:])


def unpack(pg, pz):
    g0, g1 = dups(pg)
    z0, z1 = dups(pz)
    return jnp.concatenate([g0, g1], 0), jnp.concatenate([z0, z1], 0)


def level_at(b, grp, dev):
    pos = dev if b < LOG_DEV else grp
    lev = b if b < LOG_DEV else b - LOG_DEV
    size = 32 if b < LOG_DEV else 16
    bit = lax.rem(pos // (1 << lev), 2)
    pair = size - (size >> lev) + pos // (2 << lev)
    return bit, pl.ds(pl.multiple_of(pair * 128, 128), 128)


def upper_block(b, dev_array, grp_array, at):
    return dev_array.at[0, :, at] if b < LOG_DEV else grp_array.at[:, at]


def kernel_climb(
    leaf_hbm,
    rhs_hbm,
    trans_hbm,
    dev_trans,
    grp_trans,
    inv,
    xhat,
    up_g,
    up_z,
    root_g,
    up_e,
    rhs_lo,
    rhs_hi,
    xhat_lo,
    xhat_hi,
    leaf,
    rhs,
    trans,
    grams,
    zs,
    scratch,
    outgoing,
    incoming,
    send_sem,
    recv_sem,
    halo_send,
    halo_recv,
    load_sem,
):
    grp = lax.axis_index("grp")
    dev = lax.axis_index("dev")
    place = grp * 32 + dev
    after = lax.rem(place + 1, 512)
    before = lax.rem(place + 511, 512)
    right = (after // 32, lax.rem(after, 32))
    left = (before // 32, lax.rem(before, 32))
    peers = []
    for b in range(UP):
        w = 1 << (b if b < LOG_DEV else b - LOG_DEV)
        bit, _ = level_at(b, grp, dev)
        if b < LOG_DEV:
            peers.append((grp, dev + (1 - 2 * bit) * w))
        else:
            peers.append((grp + (1 - 2 * bit) * w, dev))
    barrier = pltpu.get_barrier_semaphore()
    for peer in peers + [left, right]:
        pl.semaphore_signal(barrier, inc=1, device_id=peer, device_id_type=MESH)

    loads = [
        pltpu.make_async_copy(src, dst, load_sem.at[i])
        for i, (src, dst) in enumerate(
            [(leaf_hbm, leaf), (rhs_hbm, rhs), (trans_hbm, trans)]
            + [
                (upper_block(b, dev_trans, grp_trans, level_at(b, grp, dev)[1]), up_e.at[b])
                for b in range(UP)
            ]
        )
    ]
    for load in loads:
        load.start()

    def copy(src, dst, s, r, peer):
        return pltpu.make_async_remote_copy(
            src_ref=src,
            dst_ref=dst,
            send_sem=s,
            recv_sem=r,
            device_id=peer,
            device_id_type=MESH,
        )

    halos = [
        copy(rhs, rhs_lo, halo_send.at[0], halo_recv.at[0], right),
        copy(rhs, rhs_hi, halo_send.at[1], halo_recv.at[1], left),
        copy(xhat, xhat_lo, halo_send.at[2], halo_recv.at[2], right),
        copy(xhat, xhat_hi, halo_send.at[3], halo_recv.at[3], left),
    ]
    loads[0].wait()
    loads[1].wait()
    up_leaves(leaf, rhs, grams, zs)
    loads[2].wait()
    own_g, own_z = up_local(trans, grams, zs)
    pg, pz = pack(own_g, own_z)
    outgoing[0, 0:32, :] = pg
    outgoing[0, 32:40, :] = pz
    pl.semaphore_wait(barrier, UP + 2)
    half = lax.broadcasted_iota(jnp.int32, (64, 128), 1) // 64
    for b in range(UP):
        step = copy(
            outgoing.at[b], incoming.at[b], send_sem.at[b], recv_sem.at[b], peers[b]
        )
        step.start()
        if b == 0:
            halos[0].start()
            halos[1].start()
        if b == FILL:
            factor(grams, inv, scratch, LOC_PAIRS)
            for i in range(LOC_PAIRS):
                xhat[i] = nt(split(zs[i]), bd(split(inv[i])))
            halos[2].start()
            halos[3].start()
        mine = half == level_at(b, grp, dev)[0]
        loads[3 + b].wait()
        step.wait()
        sib_g, sib_z = unpack(incoming[b, 0:32, :], incoming[b, 32:40, :])
        g = jnp.where(mine, own_g, sib_g)
        z = jnp.where(mine[:16], own_z, sib_z)
        up_g[b] = g
        up_z[b] = z
        own_g, own_z = merge(g, z, up_e[b])
        if b + 1 < UP:
            pg, pz = pack(own_g, own_z)
            outgoing[b + 1, 0:32, :] = pg
            outgoing[b + 1, 32:40, :] = pz
    root_g[...] = own_g
    for halo in halos:
        halo.wait()


def kernel_down(
    near_partner,
    far_partner,
    up_g,
    up_z,
    root_g,
    up_e,
    dev_couple,
    grp_couple,
    leaf_hbm,
    rhs_hbm,
    rhs_lo_hbm,
    rhs_hi_hbm,
    near_hbm,
    trans_hbm,
    couple_hbm,
    inv_hbm,
    xhat_hbm,
    xhat_lo_hbm,
    xhat_hi_hbm,
    product,
    root,
    leaf,
    rhs,
    rhs_lo,
    rhs_hi,
    near,
    trans,
    couple,
    inv,
    xhat,
    xhat_lo,
    xhat_hi,
    up_s,
    grams,
    up_inv,
    scratch,
    points,
    nodes,
    load_sem,
):
    grp = lax.axis_index("grp")
    dev = lax.axis_index("dev")
    first = grp * 32 + dev - 1
    loads = [
        pltpu.make_async_copy(src, dst, load_sem.at[i])
        for i, (src, dst) in enumerate(
            [
                (upper_block(b, dev_couple, grp_couple, level_at(b, grp, dev)[1]), up_s.at[b])
                for b in range(UP)
            ]
            + [
                (rhs_hbm, rhs),
                (rhs_lo_hbm, rhs_lo),
                (rhs_hi_hbm, rhs_hi),
                (xhat_hbm, xhat),
                (xhat_lo_hbm, xhat_lo),
                (xhat_hi_hbm, xhat_hi),
                (couple_hbm, couple),
                (inv_hbm, inv),
                (trans_hbm, trans),
                (near_hbm, near),
                (leaf_hbm, leaf),
            ]
        )
    ]
    for load in loads:
        load.start()
    half = lax.broadcasted_iota(jnp.int32, (16, 128), 1) // 64
    for i in range(UP):
        grams[i] = up_g[i]
    grams[UP] = root_g[...]
    factor(grams, up_inv, scratch, UP + 1)
    upper = lax.broadcasted_iota(jnp.int32, (64, 128), 0) <= lax.broadcasted_iota(
        jnp.int32, (64, 128), 1
    )
    root[...] = jnp.where(upper, scratch[2 * UP + 1], 0.0)[:, :64].T
    for load in loads:
        load.wait()

    for s, block in enumerate((rhs_lo, rhs, rhs_hi)):
        for j in range(8):
            a, b = dups(block[:, lanes(j)])
            points[16 * s + 2 * j] = a
            points[16 * s + 2 * j + 1] = b
    for k in range(4):
        size = 16 >> k
        for s, block in enumerate((xhat_lo, xhat, xhat_hi)):
            for j in range(size // 2):
                a, b = dups(block[PAIR_BASE[k] + j])
                at = 6 * PAIR_BASE[k] + size * s + 2 * j
                nodes[at] = a
                nodes[at + 1] = b

    lifts = []
    for b in range(UP):
        bi = bd(split(up_inv[b]))
        x = swap(nt(split(up_z[b]), bi))
        lifts.append(nn(split(nt(split(x), bd(split(up_s[b])))), bi))
    v = None
    for b in reversed(range(UP)):
        t = lifts[b]
        if v is not None:
            t = t + nt(split(v), bd(split(up_e[b])))
        v = jnp.where(half == level_at(b, grp, dev)[0], t, swap(t))

    held = [v]
    for k in reversed(range(4)):
        base = PAIR_BASE[k]
        start = 6 * base - first * (16 >> k)
        grown = []
        for i in range(8 >> k):
            p = base + i
            x = pick(
                nodes[start + far_partner[0, 2 * p]], nodes[start + far_partner[0, 2 * p + 1]]
            )
            y = nt(split(x), bd(split(couple[:, lanes(p)])))
            t = nn(split(y), bd(split(inv[p])))
            t = t + nt(split(held[i]), bd(split(trans[:, lanes(p)])))
            if k > 0:
                grown.extend(dups(t))
            else:
                far = nt(split(t), bd(split(leaf[:, lanes(i)])))
                cat = jnp.concatenate(
                    [
                        pick(points[16 + 2 * i + s], points[near_partner[2 * i + s] - first * 16])
                        for s in range(2)
                    ],
                    0,
                )
                d = jnp.concatenate([near[:, lanes(2 * i)], near[:, lanes(2 * i + 1)]], 0)
                o = nt(split(cat), split(d))
                product[:, lanes(i)] = pick(o[:16], o[16:]) + far
        held = grown


def shards(
    rhs,
    leaf_basis,
    near_blocks,
    near_partner,
    local_transfer,
    local_coupling,
    far_partner,
    dev_transfer,
    dev_coupling,
    grp_transfer,
    grp_coupling,
):
    vmem = pl.BlockSpec(memory_space=pltpu.VMEM)
    smem = pl.BlockSpec(memory_space=pltpu.SMEM)
    anywhere = pl.BlockSpec(memory_space=pl.ANY)

    def shape(*dims):
        return jax.ShapeDtypeStruct(dims, f32)

    def buffer(*dims):
        return pltpu.VMEM(dims, f32)

    inv, xhat, up_g, up_z, root_g, up_e, rhs_lo, rhs_hi, xhat_lo, xhat_hi = pl.pallas_call(
        kernel_climb,
        name="climb",
        out_shape=(
            shape(15, 64, 128),
            shape(15, 16, 128),
            shape(UP, 64, 128),
            shape(UP, 16, 128),
            shape(64, 128),
            shape(UP, 64, 128),
            shape(16, 1024),
            shape(16, 1024),
            shape(15, 16, 128),
            shape(15, 16, 128),
        ),
        in_specs=[anywhere] * 5,
        out_specs=(vmem,) * 10,
        scratch_shapes=[
            buffer(64, 1024),
            buffer(16, 1024),
            buffer(64, 1920),
            buffer(15, 64, 128),
            buffer(15, 16, 128),
            buffer(30, 64, 128),
            buffer(UP, 40, 128),
            buffer(UP, 40, 128),
            pltpu.SemaphoreType.DMA((UP,)),
            pltpu.SemaphoreType.DMA((UP,)),
            pltpu.SemaphoreType.DMA((4,)),
            pltpu.SemaphoreType.DMA((4,)),
            pltpu.SemaphoreType.DMA((UP + 3,)),
        ],
        compiler_params=pltpu.CompilerParams(collective_id=0, has_side_effects=True),
    )(leaf_basis, rhs, local_transfer, dev_transfer, grp_transfer)

    return pl.pallas_call(
        kernel_down,
        name="down",
        out_shape=(shape(16, 1024), shape(64, 64)),
        in_specs=[smem] * 2 + [vmem] * 4 + [anywhere] * 13,
        out_specs=(vmem,) * 2,
        scratch_shapes=[
            buffer(64, 1024),
            buffer(16, 1024),
            buffer(16, 1024),
            buffer(16, 1024),
            buffer(64, 2048),
            buffer(64, 1920),
            buffer(64, 1920),
            buffer(15, 64, 128),
            buffer(15, 16, 128),
            buffer(15, 16, 128),
            buffer(15, 16, 128),
            buffer(UP, 64, 128),
            buffer(UP + 1, 64, 128),
            buffer(UP + 1, 64, 128),
            buffer(2 * UP + 2, 64, 128),
            buffer(48, 16, 128),
            buffer(90, 16, 128),
            pltpu.SemaphoreType.DMA((UP + 11,)),
        ],
    )(
        near_partner,
        far_partner,
        up_g,
        up_z,
        root_g,
        up_e,
        dev_coupling,
        grp_coupling,
        leaf_basis,
        rhs,
        rhs_lo,
        rhs_hi,
        near_blocks,
        local_transfer,
        local_coupling,
        inv,
        xhat,
        xhat_lo,
        xhat_hi,
    )


def solution(mesh):
    return jax.shard_map(
        shards,
        mesh=mesh,
        in_specs=(
            P(None, ("grp", "dev")),
            P(None, ("grp", "dev")),
            P(None, ("grp", "dev")),
            P(("grp", "dev")),
            P(None, ("grp", "dev")),
            P(None, ("grp", "dev")),
            P(("grp", "dev"), None),
            P("grp", None, None),
            P("grp", None, None),
            P(),
            P(),
        ),
        out_specs=(P(None, ("grp", "dev")), P()),
        check_vma=False,
    )
```

```python
import jax
import jax.numpy as jnp
from jax import lax
from jax.experimental import pallas as pl
from jax.experimental.pallas import tpu as pltpu
from jax.sharding import PartitionSpec as P

RANK = 64
NRHS = 16
LOC_PAIRS = 15
PAIR_BASE = (0, 8, 12, 14)
LOG_DEV = 5
LOG_GRP = 4
UP = LOG_DEV + LOG_GRP
ROUNDS = ((0,), (1, 2), (3, 4), (5, 6), (7, 8))
MESSAGES = 13
MESH = pl.DeviceIdType.MESH
f32 = jnp.float32
bf16 = jnp.bfloat16


def split(x):
    hi = x.astype(bf16)
    return hi, (x - hi.astype(f32)).astype(bf16)


def mm(a, b, ca, cb):
    return lax.dot_general(
        jnp.concatenate([a[0], a[1], a[0]], axis=ca),
        jnp.concatenate([b[0], b[0], b[1]], axis=cb),
        (((ca,), (cb,)), ((), ())),
        preferred_element_type=f32,
    )


def nn(a, b):
    return mm(a, b, 1, 0)


def nt(a, b):
    return mm(a, b, 1, 1)


def tn(a, b):
    return mm(a, b, 0, 0)


def left_of(rows):
    return lax.broadcasted_iota(jnp.int32, (rows, 128), 1) < 64


def swap(p):
    return pltpu.roll(p, 64, 1)


def fold(p):
    return p + swap(p)


def pick(a, b):
    return jnp.where(left_of(a.shape[0]), a, b)


def bd(pair):
    keep = left_of(64).astype(f32)
    left = keep.astype(bf16)
    right = (1.0 - keep).astype(bf16)
    return tuple(jnp.concatenate([x * left, x * right], axis=0) for x in pair)


def diag(c):
    return pick(c[:64], c[64:])


def dups(p):
    s = swap(p)
    return pick(p, s), pick(s, p)


def merge(g, z, e):
    es = split(e)
    lhs = tuple(jnp.concatenate([a, b], axis=0) for a, b in zip(bd(split(g)), split(z)))
    both = nn(lhs, bd(es))
    return fold(diag(tn(es, split(diag(both[:128]))))), fold(both[128:])


def across_rows(tile, row):
    at = jnp.full((8, 128), row, jnp.int32)
    return jnp.take_along_axis(tile, at, axis=0, mode="promise_in_bounds")


def stacked_blocks(wide, parts):
    lane = lax.broadcasted_iota(jnp.int32, (32, 128), 1) // 32
    keeps = [jnp.where(lane == q, 1.0, 0.0).astype(bf16) for q in range(4)]
    return tuple(
        jnp.concatenate([x[p : p + 32] * k for p, k in zip(parts, keeps)], axis=0)
        for x in split(wide)
    )


def eliminate(a, start):
    row = lax.broadcasted_iota(jnp.int32, (8, 128), 0)
    lane = lax.broadcasted_iota(jnp.int32, (8, 128), 1)
    out = [start[t] for t in range(4)]
    for j in range(0, 32, 2):
        h, js = j // 8, j % 8
        below = row > js + 1
        at = lane // 32 * 32 + j

        def across(tile, where):
            return jnp.take_along_axis(tile, where, axis=1, mode="promise_in_bounds")

        first = {t: across(a[t], at) for t in range(h, 4)}
        second = {t: across(a[t], at + 1) for t in range(h, 4)}
        yield
        i0 = lax.rsqrt(across_rows(first[h], js))
        q = across_rows(second[h], js) * i0
        i1 = lax.rsqrt(across_rows(second[h], js + 1) - q * q)
        top0 = across_rows(a[h], js) * i0
        top1 = (across_rows(a[h], js + 1) - q * top0) * i1
        eye0 = across_rows(out[h], js) * i0
        eye1 = (across_rows(out[h], js + 1) - q * eye0) * i1
        for t in range(h, 4):
            if t > h or js < 6:
                m0 = first[t] * i0
                m1 = (second[t] - m0 * q) * i1
                if t == h:
                    m0 = jnp.where(below, m0, 0.0)
                    m1 = jnp.where(below, m1, 0.0)
                a[t] = a[t] - m0 * top0 - m1 * top1
                out[t] = out[t] - m0 * eye0 - m1 * eye1
        out[h] = jnp.where(row == js, eye0, jnp.where(row == js + 1, eye1, out[h]))
        yield
    a[:] = out


def factor(grams, inverses, scratch, pairs):
    row = lax.broadcasted_iota(jnp.int32, (64, 128), 0)
    lane = lax.broadcasted_iota(jnp.int32, (64, 128), 1)
    left = lane < 64
    eye_left = jnp.where(row == lane, 1.0, 0.0)
    eye_right = jnp.where(row == lane - 64, 1.0, 0.0)
    for p in range(pairs):
        s = swap(grams[p])
        scratch[2 * p] = jnp.where(left, eye_left, s)
        scratch[2 * p + 1] = jnp.where(left, s, eye_right)
    nodes = 2 * pairs
    groups = []
    for g in range(0, nodes, 4):
        groups.append([g + q if g + q < nodes else g + q % 2 for q in range(4)])
    eyes = [
        jnp.where(
            lax.broadcasted_iota(jnp.int32, (8, 128), 0) + 8 * t
            == lax.broadcasted_iota(jnp.int32, (8, 128), 1) % 32,
            1.0,
            0.0,
        )
        for t in range(4)
    ]
    for lo in (0, 32):
        packs = []
        for members in groups:
            tiles = []
            for t in range(4):
                tile = None
                for q, n in enumerate(members):
                    shift = (32 * q - lo - (64 if n % 2 == 0 else 0)) % 128
                    x = scratch[n, lo + 8 * t : lo + 8 * t + 8, :]
                    x = pltpu.roll(x, shift, 1) if shift else x
                    tile = x if q == 0 else jnp.where(lane[:8] // 32 == q, x, tile)
                tiles.append(tile)
            packs.append(tiles)
        running = [eliminate(tiles, eyes) for tiles in packs]
        for _ in range(33):
            for run in running:
                next(run, None)
        for members, tiles in zip(groups, packs):
            rows = jnp.concatenate([scratch[n, lo : lo + 32, :] for n in members], axis=0)
            solved = nn(
                stacked_blocks(jnp.concatenate(tiles, axis=0), (0, 0, 0, 0)), split(rows)
            )
            if lo == 0:
                parts = [96 if n % 2 == 0 else 32 for n in members]
                change = nn(stacked_blocks(solved.T, parts), split(solved))
            for q, n in enumerate(members):
                if n == members[0] + q:
                    scratch[n, lo : lo + 32, :] = solved[32 * q : 32 * q + 32]
                    if lo == 0:
                        scratch[n, 32:64, :] -= change[32 * q : 32 * q + 32]
    for p in range(pairs):
        inverses[p] = jnp.where(left, scratch[2 * p], scratch[2 * p + 1])


def lanes(i):
    return slice(128 * i, 128 * i + 128)


def up_leaves(leaf, rhs, grams, zs):
    for j in range(8):
        u = split(leaf[:, lanes(j)])
        grams[j] = diag(tn(u, u))
        zs[j] = nn(split(rhs[:, lanes(j)]), bd(u))


def up_local(trans, grams, zs):
    for k in range(4):
        base = PAIR_BASE[k]
        held = None
        for i in range(8 >> k):
            g, z = merge(grams[base + i], zs[base + i], trans[:, lanes(base + i)])
            if k == 3:
                return g, z
            if i % 2 == 0:
                held = (g, z)
            else:
                grams[PAIR_BASE[k + 1] + i // 2] = pick(held[0], g)
                zs[PAIR_BASE[k + 1] + i // 2] = pick(held[1], z)


def pack(g, z):
    return pick(g[:32], g[32:]), pick(z[:8], z[8:])


def unpack(pg, pz):
    g0, g1 = dups(pg)
    z0, z1 = dups(pz)
    return jnp.concatenate([g0, g1], 0), jnp.concatenate([z0, z1], 0)


def spot(b, grp, dev):
    if b < LOG_DEV:
        return dev, b, 32
    return grp, b - LOG_DEV, 16


def bit_of(b, grp, dev):
    pos, lev, _ = spot(b, grp, dev)
    return lax.rem(pos // (1 << lev), 2)


def pair_block(b, grp, dev, dev_array, grp_array, other=False):
    pos, lev, size = spot(b, grp, dev)
    if other:
        pos = pos + (1 - 2 * bit_of(b + 1, grp, dev)) * (2 << lev)
    pair = size - (size >> lev) + pos // (2 << lev)
    at = pl.ds(pl.multiple_of(pair * 128, 128), 128)
    return dev_array.at[0, :, at] if b < LOG_DEV else grp_array.at[:, at]


def flipped(bits, grp, dev):
    for b in bits:
        lev = spot(b, grp, dev)[1]
        move = (1 - 2 * bit_of(b, grp, dev)) * (1 << lev)
        if b < LOG_DEV:
            dev = dev + move
        else:
            grp = grp + move
    return grp, dev


def kernel_climb(
    near_partner,
    far_partner,
    leaf_hbm,
    rhs_hbm,
    trans_hbm,
    near_hbm,
    couple_hbm,
    dev_trans,
    grp_trans,
    up_g,
    up_z,
    root_g,
    paths,
    lifts,
    base_out,
    rhs_lo,
    rhs_hi,
    xhat_lo,
    xhat_hi,
    leaf,
    rhs,
    trans,
    near,
    couple,
    inv,
    xhat,
    up_e,
    side_e,
    grams,
    zs,
    scratch,
    points,
    nodes,
    outgoing,
    incoming,
    send_sem,
    recv_sem,
    halo_send,
    halo_recv,
    load_sem,
):
    grp = lax.axis_index("grp")
    dev = lax.axis_index("dev")
    place = grp * 32 + dev
    first = place - 1
    after = lax.rem(place + 1, 512)
    before = lax.rem(place + 511, 512)
    right = (after // 32, lax.rem(after, 32))
    left = (before // 32, lax.rem(before, 32))
    barrier = pltpu.get_barrier_semaphore()
    peers = []
    for bits in ROUNDS:
        flips = [bits] if len(bits) == 1 else [bits[:1], bits[1:], bits]
        peers.append([flipped(f, grp, dev) for f in flips])
    greeted = [p for group in peers for p in group] + [left, right]
    for peer in greeted:
        pl.semaphore_signal(barrier, inc=1, device_id=peer, device_id_type=MESH)

    wanted = [(leaf_hbm, leaf), (rhs_hbm, rhs), (trans_hbm, trans)]
    for b in range(UP):
        wanted.append((pair_block(b, grp, dev, dev_trans, grp_trans), up_e.at[b]))
    for i, bits in enumerate(ROUNDS[1:]):
        wanted.append(
            (pair_block(bits[0], grp, dev, dev_trans, grp_trans, True), side_e.at[i])
        )
    wanted.extend([(near_hbm, near), (couple_hbm, couple)])
    loads = [
        pltpu.make_async_copy(s, d, load_sem.at[i]) for i, (s, d) in enumerate(wanted)
    ]
    for load in loads:
        load.start()

    def copy(src, dst, s, r, peer):
        return pltpu.make_async_remote_copy(
            src_ref=src,
            dst_ref=dst,
            send_sem=s,
            recv_sem=r,
            device_id=peer,
            device_id_type=MESH,
        )

    halos = [
        copy(rhs, rhs_lo, halo_send.at[0], halo_recv.at[0], right),
        copy(rhs, rhs_hi, halo_send.at[1], halo_recv.at[1], left),
        copy(xhat, xhat_lo, halo_send.at[2], halo_recv.at[2], right),
        copy(xhat, xhat_hi, halo_send.at[3], halo_recv.at[3], left),
    ]
    half = lax.broadcasted_iota(jnp.int32, (64, 128), 1) // 64
    mine = [half == bit_of(b, grp, dev) for b in range(UP)]

    def factor_local():
        factor(grams, inv, scratch, LOC_PAIRS)
        for i in range(LOC_PAIRS):
            xhat[i] = nt(split(zs[i]), bd(split(inv[i])))
        halos[2].start()
        halos[3].start()

    def near_field():
        halos[0].wait()
        halos[1].wait()
        loads[-2].wait()
        for s, block in enumerate((rhs_lo, rhs, rhs_hi)):
            for j in range(8):
                a, b = dups(block[:, lanes(j)])
                points[16 * s + 2 * j] = a
                points[16 * s + 2 * j + 1] = b
        for i in range(8):
            cat = jnp.concatenate(
                [
                    pick(points[16 + 2 * i + s], points[jnp.clip(near_partner[2 * i + s] - first * 16, 0, 47)])
                    for s in range(2)
                ],
                0,
            )
            d = jnp.concatenate([near[:, lanes(2 * i)], near[:, lanes(2 * i + 1)]], 0)
            o = nt(split(cat), split(d))
            base_out[:, lanes(i)] = pick(o[:16], o[16:])

    def local_lifts():
        halos[2].wait()
        halos[3].wait()
        loads[-1].wait()
        for k in range(4):
            size = 16 >> k
            base = PAIR_BASE[k]
            for s, block in enumerate((xhat_lo, xhat, xhat_hi)):
                for j in range(size // 2):
                    a, b = dups(block[base + j])
                    at = 6 * base + size * s + 2 * j
                    nodes[at] = a
                    nodes[at + 1] = b
            for i in range(8 >> k):
                p = base + i
                x = pick(
                    nodes[6 * base + jnp.clip(far_partner[0, 2 * p] - first * size, 0, 3 * size - 1)],
                    nodes[6 * base + jnp.clip(far_partner[0, 2 * p + 1] - first * size, 0, 3 * size - 1)],
                )
                y = nt(split(x), bd(split(couple[:, lanes(p)])))
                lifts[p] = nn(split(y), bd(split(inv[p])))

    def extend_paths(levels):
        for b in levels:
            e = up_e[b]
            if b > 0:
                e = nn(split(paths[b - 1]), bd(split(e)))
            paths[b] = jnp.where(mine[b], e, swap(e))

    loads[0].wait()
    loads[1].wait()
    up_leaves(leaf, rhs, grams, zs)
    loads[2].wait()
    own_g, own_z = up_local(trans, grams, zs)
    for load in loads[3:-2]:
        load.wait()
    pl.semaphore_wait(barrier, len(greeted))
    slot = 0
    for r, bits in enumerate(ROUNDS):
        pg, pz = pack(own_g, own_z)
        outgoing[r, 0:32, :] = pg
        outgoing[r, 32:40, :] = pz
        steps = []
        for i, peer in enumerate(peers[r]):
            at = slot + i
            steps.append(
                copy(outgoing.at[r], incoming.at[at], send_sem.at[at], recv_sem.at[at], peer)
            )
        for step in steps:
            step.start()
        if r == 0:
            halos[0].start()
            halos[1].start()
            extend_paths((0,))
        elif r == 1:
            extend_paths((1, 2))
        elif r == 2:
            factor_local()
            extend_paths((3, 4))
        elif r == 3:
            near_field()
            extend_paths((5, 6, 7))
        else:
            local_lifts()
        for step in steps:
            step.wait()
        b = bits[0]
        got = [
            unpack(incoming[slot + i, 0:32, :], incoming[slot + i, 32:40, :])
            for i in range(len(steps))
        ]
        slot += len(steps)
        g = jnp.where(mine[b], own_g, got[0][0])
        z = jnp.where(mine[b][:16], own_z, got[0][1])
        up_g[b] = g
        up_z[b] = z
        own_g, own_z = merge(g, z, up_e[b])
        if len(bits) == 2:
            g = jnp.where(mine[b], got[1][0], got[2][0])
            z = jnp.where(mine[b][:16], got[1][1], got[2][1])
            side_g, side_z = merge(g, z, side_e[r - 1])
            g = jnp.where(mine[b + 1], own_g, side_g)
            z = jnp.where(mine[b + 1][:16], own_z, side_z)
            up_g[b + 1] = g
            up_z[b + 1] = z
            own_g, own_z = merge(g, z, up_e[b + 1])
    root_g[...] = own_g


def kernel_down(
    up_g,
    up_z,
    root_g,
    paths,
    lifts,
    base_in,
    dev_couple,
    grp_couple,
    leaf_hbm,
    trans_hbm,
    product,
    root,
    leaf,
    trans,
    up_s,
    grams,
    up_inv,
    scratch,
    load_sem,
):
    grp = lax.axis_index("grp")
    dev = lax.axis_index("dev")
    wanted = [
        (pair_block(b, grp, dev, dev_couple, grp_couple), up_s.at[b]) for b in range(UP)
    ]
    wanted.extend([(trans_hbm, trans), (leaf_hbm, leaf)])
    loads = [
        pltpu.make_async_copy(s, d, load_sem.at[i]) for i, (s, d) in enumerate(wanted)
    ]
    for load in loads:
        load.start()
    half = lax.broadcasted_iota(jnp.int32, (16, 128), 1) // 64
    for i in range(UP):
        grams[i] = up_g[i]
    grams[UP] = root_g[...]
    factor(grams, up_inv, scratch, UP + 1)
    upper = lax.broadcasted_iota(jnp.int32, (64, 128), 0) <= lax.broadcasted_iota(
        jnp.int32, (64, 128), 1
    )
    root[...] = jnp.where(upper, scratch[2 * UP + 1], 0.0)[:, :64].T
    for load in loads:
        load.wait()

    v = None
    for b in range(UP):
        bi = bd(split(up_inv[b]))
        x = swap(nt(split(up_z[b]), bi))
        t = nn(split(nt(split(x), bd(split(up_s[b])))), bi)
        t = jnp.where(half == bit_of(b, grp, dev), t, swap(t))
        if b == 0:
            v = t
        else:
            path = tuple(jnp.concatenate([x, x], axis=0) for x in split(paths[b - 1]))
            v = v + nt(split(jnp.where(half == 0, t, 0.0)), path)

    held = [v]
    for k in reversed(range(4)):
        grown = []
        for i in range(8 >> k):
            p = PAIR_BASE[k] + i
            t = lifts[p] + nt(split(held[i]), bd(split(trans[:, lanes(p)])))
            if k > 0:
                grown.extend(dups(t))
            else:
                far = nt(split(t), bd(split(leaf[:, lanes(i)])))
                product[:, lanes(i)] = base_in[:, lanes(i)] + far
        held = grown


def shards(
    rhs,
    leaf_basis,
    near_blocks,
    near_partner,
    local_transfer,
    local_coupling,
    far_partner,
    dev_transfer,
    dev_coupling,
    grp_transfer,
    grp_coupling,
):
    vmem = pl.BlockSpec(memory_space=pltpu.VMEM)
    smem = pl.BlockSpec(memory_space=pltpu.SMEM)
    anywhere = pl.BlockSpec(memory_space=pl.ANY)

    def shape(*dims):
        return jax.ShapeDtypeStruct(dims, f32)

    def buffer(*dims):
        return pltpu.VMEM(dims, f32)

    handed = pl.pallas_call(
        kernel_climb,
        name="climb",
        out_shape=(
            shape(UP, 64, 128),
            shape(UP, 16, 128),
            shape(64, 128),
            shape(UP - 1, 64, 128),
            shape(15, 16, 128),
            shape(16, 1024),
        ),
        in_specs=[smem] * 2 + [anywhere] * 7,
        out_specs=(vmem,) * 6,
        scratch_shapes=[
            buffer(16, 1024),
            buffer(16, 1024),
            buffer(15, 16, 128),
            buffer(15, 16, 128),
            buffer(64, 1024),
            buffer(16, 1024),
            buffer(64, 1920),
            buffer(64, 2048),
            buffer(64, 1920),
            buffer(15, 64, 128),
            buffer(15, 16, 128),
            buffer(UP, 64, 128),
            buffer(len(ROUNDS) - 1, 64, 128),
            buffer(15, 64, 128),
            buffer(15, 16, 128),
            buffer(30, 64, 128),
            buffer(48, 16, 128),
            buffer(90, 16, 128),
            buffer(len(ROUNDS), 40, 128),
            buffer(MESSAGES, 40, 128),
            pltpu.SemaphoreType.DMA((MESSAGES,)),
            pltpu.SemaphoreType.DMA((MESSAGES,)),
            pltpu.SemaphoreType.DMA((4,)),
            pltpu.SemaphoreType.DMA((4,)),
            pltpu.SemaphoreType.DMA((UP + len(ROUNDS) + 4,)),
        ],
        compiler_params=pltpu.CompilerParams(collective_id=0, has_side_effects=True),
    )(
        near_partner,
        far_partner,
        leaf_basis,
        rhs,
        local_transfer,
        near_blocks,
        local_coupling,
        dev_transfer,
        grp_transfer,
    )

    return pl.pallas_call(
        kernel_down,
        name="down",
        out_shape=(shape(16, 1024), shape(64, 64)),
        in_specs=[vmem] * 6 + [anywhere] * 4,
        out_specs=(vmem,) * 2,
        scratch_shapes=[
            buffer(64, 1024),
            buffer(64, 1920),
            buffer(UP, 64, 128),
            buffer(UP + 1, 64, 128),
            buffer(UP + 1, 64, 128),
            buffer(2 * UP + 2, 64, 128),
            pltpu.SemaphoreType.DMA((UP + 2,)),
        ],
    )(*handed, dev_coupling, grp_coupling, leaf_basis, local_transfer)


def solution(mesh):
    return jax.shard_map(
        shards,
        mesh=mesh,
        in_specs=(
            P(None, ("grp", "dev")),
            P(None, ("grp", "dev")),
            P(None, ("grp", "dev")),
            P(("grp", "dev")),
            P(None, ("grp", "dev")),
            P(None, ("grp", "dev")),
            P(("grp", "dev"), None),
            P("grp", None, None),
            P("grp", None, None),
            P(),
            P(),
        ),
        out_specs=(P(None, ("grp", "dev")), P()),
        check_vma=False,
    )
```

```python
import jax
import jax.numpy as jnp
from jax import lax
from jax.experimental import pallas as pl
from jax.experimental.pallas import tpu as pltpu
from jax.sharding import PartitionSpec as P

RANK = 64
NRHS = 16
LOC_PAIRS = 15
PAIR_BASE = (0, 8, 12, 14)
LOG_DEV = 5
LOG_GRP = 4
UP = LOG_DEV + LOG_GRP
ROUNDS = ((0,), (1, 2), (3, 4), (5, 6), (7, 8))
MESSAGES = 13
MESH = pl.DeviceIdType.MESH
f32 = jnp.float32
bf16 = jnp.bfloat16


def split(x):
    hi = x.astype(bf16)
    return hi, (x - hi.astype(f32)).astype(bf16)


def mm(a, b, ca, cb):
    return lax.dot_general(
        jnp.concatenate([a[0], a[1], a[0]], axis=ca),
        jnp.concatenate([b[0], b[0], b[1]], axis=cb),
        (((ca,), (cb,)), ((), ())),
        preferred_element_type=f32,
    )


def nn(a, b):
    return mm(a, b, 1, 0)


def nt(a, b):
    return mm(a, b, 1, 1)


def tn(a, b):
    return mm(a, b, 0, 0)


def left_of(rows):
    return lax.broadcasted_iota(jnp.int32, (rows, 128), 1) < 64


def swap(p):
    return pltpu.roll(p, 64, 1)


def fold(p):
    return p + swap(p)


def pick(a, b):
    return jnp.where(left_of(a.shape[0]), a, b)


def bd(pair):
    keep = left_of(64).astype(f32)
    left = keep.astype(bf16)
    right = (1.0 - keep).astype(bf16)
    return tuple(jnp.concatenate([x * left, x * right], axis=0) for x in pair)


def diag(c):
    return pick(c[:64], c[64:])


def dups(p):
    s = swap(p)
    return pick(p, s), pick(s, p)


def merge(g, z, e):
    es = split(e)
    both = nn(split(jnp.concatenate([g, z], axis=0)), bd(es))
    return fold(diag(tn(es, split(both[:64])))), fold(both[64:])


def across_rows(tile, row):
    at = jnp.full((8, 128), row, jnp.int32)
    return jnp.take_along_axis(tile, at, axis=0, mode="promise_in_bounds")


def stacked_blocks(wide, parts):
    lane = lax.broadcasted_iota(jnp.int32, (32, 128), 1) // 32
    keeps = [jnp.where(lane == q, 1.0, 0.0).astype(bf16) for q in range(4)]
    return tuple(
        jnp.concatenate([x[p : p + 32] * k for p, k in zip(parts, keeps)], axis=0)
        for x in split(wide)
    )


def eliminate(a, start):
    row = lax.broadcasted_iota(jnp.int32, (8, 128), 0)
    lane = lax.broadcasted_iota(jnp.int32, (8, 128), 1)
    out = [start[t] for t in range(4)]
    for j in range(0, 32, 2):
        h, js = j // 8, j % 8
        below = row > js + 1
        at = lane // 32 * 32 + j

        def across(tile, where):
            return jnp.take_along_axis(tile, where, axis=1, mode="promise_in_bounds")

        first = {t: across(a[t], at) for t in range(h, 4)}
        second = {t: across(a[t], at + 1) for t in range(h, 4)}
        yield
        i0 = lax.rsqrt(across_rows(first[h], js))
        q = across_rows(second[h], js) * i0
        i1 = lax.rsqrt(across_rows(second[h], js + 1) - q * q)
        top0 = across_rows(a[h], js) * i0
        top1 = (across_rows(a[h], js + 1) - q * top0) * i1
        eye0 = across_rows(out[h], js) * i0
        eye1 = (across_rows(out[h], js + 1) - q * eye0) * i1
        for t in range(h, 4):
            if t > h or js < 6:
                m0 = first[t] * i0
                m1 = (second[t] - m0 * q) * i1
                if t == h:
                    m0 = jnp.where(below, m0, 0.0)
                    m1 = jnp.where(below, m1, 0.0)
                a[t] = a[t] - m0 * top0 - m1 * top1
                out[t] = out[t] - m0 * eye0 - m1 * eye1
        out[h] = jnp.where(row == js, eye0, jnp.where(row == js + 1, eye1, out[h]))
        yield
    a[:] = out


def factor(grams, inverses, scratch, pairs):
    row = lax.broadcasted_iota(jnp.int32, (64, 128), 0)
    lane = lax.broadcasted_iota(jnp.int32, (64, 128), 1)
    left = lane < 64
    eye_left = jnp.where(row == lane, 1.0, 0.0)
    eye_right = jnp.where(row == lane - 64, 1.0, 0.0)
    for p in range(pairs):
        s = swap(grams[p])
        scratch[2 * p] = jnp.where(left, eye_left, s)
        scratch[2 * p + 1] = jnp.where(left, s, eye_right)
    nodes = 2 * pairs
    groups = []
    for g in range(0, nodes, 4):
        groups.append([g + q if g + q < nodes else g + q % 2 for q in range(4)])
    eyes = [
        jnp.where(
            lax.broadcasted_iota(jnp.int32, (8, 128), 0) + 8 * t
            == lax.broadcasted_iota(jnp.int32, (8, 128), 1) % 32,
            1.0,
            0.0,
        )
        for t in range(4)
    ]
    for lo in (0, 32):
        packs = []
        for members in groups:
            tiles = []
            for t in range(4):
                tile = None
                for q, n in enumerate(members):
                    shift = (32 * q - lo - (64 if n % 2 == 0 else 0)) % 128
                    x = scratch[n, lo + 8 * t : lo + 8 * t + 8, :]
                    x = pltpu.roll(x, shift, 1) if shift else x
                    tile = x if q == 0 else jnp.where(lane[:8] // 32 == q, x, tile)
                tiles.append(tile)
            packs.append(tiles)
        running = [eliminate(tiles, eyes) for tiles in packs]
        for _ in range(33):
            for run in running:
                next(run, None)
        for members, tiles in zip(groups, packs):
            rows = jnp.concatenate([scratch[n, lo : lo + 32, :] for n in members], axis=0)
            solved = nn(
                stacked_blocks(jnp.concatenate(tiles, axis=0), (0, 0, 0, 0)), split(rows)
            )
            if lo == 0:
                parts = [96 if n % 2 == 0 else 32 for n in members]
                change = nn(stacked_blocks(solved.T, parts), split(solved))
            for q, n in enumerate(members):
                if n == members[0] + q:
                    scratch[n, lo : lo + 32, :] = solved[32 * q : 32 * q + 32]
                    if lo == 0:
                        scratch[n, 32:64, :] -= change[32 * q : 32 * q + 32]
    for p in range(pairs):
        inverses[p] = jnp.where(left, scratch[2 * p], scratch[2 * p + 1])


def lanes(i):
    return slice(128 * i, 128 * i + 128)


def up_leaves(leaf, rhs, grams, zs):
    for j in range(8):
        u = split(leaf[:, lanes(j)])
        grams[j] = diag(tn(u, u))
        zs[j] = nn(split(rhs[:, lanes(j)]), bd(u))


def up_local(trans, grams, zs):
    for k in range(4):
        base = PAIR_BASE[k]
        held = None
        for i in range(8 >> k):
            g, z = merge(grams[base + i], zs[base + i], trans[:, lanes(base + i)])
            if k == 3:
                return g, z
            if i % 2 == 0:
                held = (g, z)
            else:
                grams[PAIR_BASE[k + 1] + i // 2] = pick(held[0], g)
                zs[PAIR_BASE[k + 1] + i // 2] = pick(held[1], z)


def pack(g, z):
    return pick(g[:32], g[32:]), pick(z[:8], z[8:])


def unpack(pg, pz):
    g0, g1 = dups(pg)
    z0, z1 = dups(pz)
    return jnp.concatenate([g0, g1], 0), jnp.concatenate([z0, z1], 0)


def spot(b, grp, dev):
    if b < LOG_DEV:
        return dev, b, 32
    return grp, b - LOG_DEV, 16


def bit_of(b, grp, dev):
    pos, lev, _ = spot(b, grp, dev)
    return lax.rem(pos // (1 << lev), 2)


def pair_block(b, grp, dev, dev_array, grp_array, other=False):
    pos, lev, size = spot(b, grp, dev)
    if other:
        pos = pos + (1 - 2 * bit_of(b + 1, grp, dev)) * (2 << lev)
    pair = size - (size >> lev) + pos // (2 << lev)
    at = pl.ds(pl.multiple_of(pair * 128, 128), 128)
    return dev_array.at[0, :, at] if b < LOG_DEV else grp_array.at[:, at]


def flipped(bits, grp, dev):
    for b in bits:
        lev = spot(b, grp, dev)[1]
        move = (1 - 2 * bit_of(b, grp, dev)) * (1 << lev)
        if b < LOG_DEV:
            dev = dev + move
        else:
            grp = grp + move
    return grp, dev


def kernel_climb(
    near_partner,
    far_partner,
    leaf_hbm,
    rhs_hbm,
    trans_hbm,
    near_hbm,
    couple_hbm,
    dev_trans,
    grp_trans,
    dev_couple,
    grp_couple,
    product,
    root,
    up_g,
    up_z,
    up_s,
    up_inv,
    paths,
    lifts,
    base_out,
    rhs_lo,
    rhs_hi,
    xhat_lo,
    xhat_hi,
    leaf,
    rhs,
    trans,
    near,
    couple,
    inv,
    xhat,
    up_e,
    side_e,
    grams,
    zs,
    scratch,
    points,
    nodes,
    outgoing,
    incoming,
    send_sem,
    recv_sem,
    halo_send,
    halo_recv,
    load_sem,
):
    grp = lax.axis_index("grp")
    dev = lax.axis_index("dev")
    place = grp * 32 + dev
    first = place - 1
    after = lax.rem(place + 1, 512)
    before = lax.rem(place + 511, 512)
    right = (after // 32, lax.rem(after, 32))
    left = (before // 32, lax.rem(before, 32))
    barrier = pltpu.get_barrier_semaphore()
    peers = []
    for bits in ROUNDS:
        flips = [bits] if len(bits) == 1 else [bits[:1], bits[1:], bits]
        peers.append([flipped(f, grp, dev) for f in flips])
    greeted = [p for group in peers for p in group] + [left, right]
    for peer in greeted:
        pl.semaphore_signal(barrier, inc=1, device_id=peer, device_id_type=MESH)

    wanted = [(leaf_hbm, leaf), (rhs_hbm, rhs), (trans_hbm, trans)]
    for b in range(UP):
        wanted.append((pair_block(b, grp, dev, dev_trans, grp_trans), up_e.at[b]))
    for i, bits in enumerate(ROUNDS[1:]):
        wanted.append(
            (pair_block(bits[0], grp, dev, dev_trans, grp_trans, True), side_e.at[i])
        )
    for b in range(UP):
        wanted.append((pair_block(b, grp, dev, dev_couple, grp_couple), up_s.at[b]))
    wanted.extend([(near_hbm, near), (couple_hbm, couple)])
    loads = [
        pltpu.make_async_copy(s, d, load_sem.at[i]) for i, (s, d) in enumerate(wanted)
    ]
    for load in loads:
        load.start()

    def copy(src, dst, s, r, peer):
        return pltpu.make_async_remote_copy(
            src_ref=src,
            dst_ref=dst,
            send_sem=s,
            recv_sem=r,
            device_id=peer,
            device_id_type=MESH,
        )

    halos = [
        copy(rhs, rhs_lo, halo_send.at[0], halo_recv.at[0], right),
        copy(rhs, rhs_hi, halo_send.at[1], halo_recv.at[1], left),
        copy(xhat, xhat_lo, halo_send.at[2], halo_recv.at[2], right),
        copy(xhat, xhat_hi, halo_send.at[3], halo_recv.at[3], left),
    ]
    half = lax.broadcasted_iota(jnp.int32, (64, 128), 1) // 64
    mine = [half == bit_of(b, grp, dev) for b in range(UP)]

    def factor_local():
        factor(grams, inv, scratch, LOC_PAIRS)
        for i in range(LOC_PAIRS):
            xhat[i] = nt(split(zs[i]), bd(split(inv[i])))
        halos[2].start()
        halos[3].start()

    def near_field():
        halos[0].wait()
        halos[1].wait()
        loads[-2].wait()
        for s, block in enumerate((rhs_lo, rhs, rhs_hi)):
            for j in range(8):
                a, b = dups(block[:, lanes(j)])
                points[16 * s + 2 * j] = a
                points[16 * s + 2 * j + 1] = b
        for i in range(8):
            cat = jnp.concatenate(
                [
                    pick(points[16 + 2 * i + s], points[jnp.clip(near_partner[2 * i + s] - first * 16, 0, 47)])
                    for s in range(2)
                ],
                0,
            )
            d = jnp.concatenate([near[:, lanes(2 * i)], near[:, lanes(2 * i + 1)]], 0)
            o = nt(split(cat), split(d))
            base_out[:, lanes(i)] = pick(o[:16], o[16:])

    def local_lifts():
        halos[2].wait()
        halos[3].wait()
        loads[-1].wait()
        for k in range(4):
            size = 16 >> k
            base = PAIR_BASE[k]
            for s, block in enumerate((xhat_lo, xhat, xhat_hi)):
                for j in range(size // 2):
                    a, b = dups(block[base + j])
                    at = 6 * base + size * s + 2 * j
                    nodes[at] = a
                    nodes[at + 1] = b
            for i in range(8 >> k):
                p = base + i
                x = pick(
                    nodes[6 * base + jnp.clip(far_partner[0, 2 * p] - first * size, 0, 3 * size - 1)],
                    nodes[6 * base + jnp.clip(far_partner[0, 2 * p + 1] - first * size, 0, 3 * size - 1)],
                )
                y = nt(split(x), bd(split(couple[:, lanes(p)])))
                lifts[p] = nn(split(y), bd(split(inv[p])))

    def extend_paths(levels):
        for b in levels:
            e = up_e[b]
            if b > 0:
                e = nn(split(paths[b - 1]), bd(split(e)))
            paths[b] = jnp.where(mine[b], e, swap(e))

    loads[0].wait()
    loads[1].wait()
    up_leaves(leaf, rhs, grams, zs)
    loads[2].wait()
    own_g, own_z = up_local(trans, grams, zs)
    for load in loads[3:-2]:
        load.wait()
    pl.semaphore_wait(barrier, len(greeted))
    slot = 0
    for r, bits in enumerate(ROUNDS):
        pg, pz = pack(own_g, own_z)
        outgoing[r, 0:32, :] = pg
        outgoing[r, 32:40, :] = pz
        steps = []
        for i, peer in enumerate(peers[r]):
            at = slot + i
            steps.append(
                copy(outgoing.at[r], incoming.at[at], send_sem.at[at], recv_sem.at[at], peer)
            )
        for step in steps:
            step.start()
        if r == 0:
            halos[0].start()
            halos[1].start()
            extend_paths((0,))
        elif r == 1:
            extend_paths((1, 2))
        elif r == 2:
            factor_local()
            extend_paths((3, 4))
        elif r == 3:
            near_field()
            extend_paths((5, 6, 7))
        else:
            local_lifts()
        for step in steps:
            step.wait()
        b = bits[0]
        got = [
            unpack(incoming[slot + i, 0:32, :], incoming[slot + i, 32:40, :])
            for i in range(len(steps))
        ]
        slot += len(steps)
        g = jnp.where(mine[b], own_g, got[0][0])
        z = jnp.where(mine[b][:16], own_z, got[0][1])
        up_g[b] = g
        up_z[b] = z
        own_g, own_z = merge(g, z, up_e[b])
        if len(bits) == 2:
            g = jnp.where(mine[b], got[1][0], got[2][0])
            z = jnp.where(mine[b][:16], got[1][1], got[2][1])
            side_g, side_z = merge(g, z, side_e[r - 1])
            g = jnp.where(mine[b + 1], own_g, side_g)
            z = jnp.where(mine[b + 1][:16], own_z, side_z)
            up_g[b + 1] = g
            up_z[b + 1] = z
            own_g, own_z = merge(g, z, up_e[b + 1])
    up_g[UP] = own_g
    side = lax.broadcasted_iota(jnp.int32, (16, 128), 1) // 64
    factor(up_g, up_inv, scratch, UP + 1)
    upper = lax.broadcasted_iota(jnp.int32, (64, 128), 0) <= lax.broadcasted_iota(
        jnp.int32, (64, 128), 1
    )
    root[...] = jnp.where(upper, scratch[2 * UP + 1], 0.0)[:, :64].T
    v = None
    for b in range(UP):
        bi = bd(split(up_inv[b]))
        x = swap(nt(split(up_z[b]), bi))
        t = nn(split(nt(split(x), bd(split(up_s[b])))), bi)
        t = jnp.where(side == bit_of(b, grp, dev), t, swap(t))
        if b == 0:
            v = t
        else:
            path = tuple(jnp.concatenate([x, x], axis=0) for x in split(paths[b - 1]))
            v = v + nt(split(jnp.where(side == 0, t, 0.0)), path)

    held = [v]
    for k in reversed(range(4)):
        grown = []
        for i in range(8 >> k):
            p = PAIR_BASE[k] + i
            t = lifts[p] + nt(split(held[i]), bd(split(trans[:, lanes(p)])))
            if k > 0:
                grown.extend(dups(t))
            else:
                far = nt(split(t), bd(split(leaf[:, lanes(i)])))
                product[:, lanes(i)] = base_out[:, lanes(i)] + far
        held = grown


def shards(
    rhs,
    leaf_basis,
    near_blocks,
    near_partner,
    local_transfer,
    local_coupling,
    far_partner,
    dev_transfer,
    dev_coupling,
    grp_transfer,
    grp_coupling,
):
    vmem = pl.BlockSpec(memory_space=pltpu.VMEM)
    smem = pl.BlockSpec(memory_space=pltpu.SMEM)
    anywhere = pl.BlockSpec(memory_space=pl.ANY)

    def shape(*dims):
        return jax.ShapeDtypeStruct(dims, f32)

    def buffer(*dims):
        return pltpu.VMEM(dims, f32)

    return pl.pallas_call(
        kernel_climb,
        name="climb",
        out_shape=(shape(16, 1024), shape(64, 64)),
        in_specs=[smem] * 2 + [anywhere] * 9,
        out_specs=(vmem,) * 2,
        scratch_shapes=[
            buffer(UP + 1, 64, 128),
            buffer(UP, 16, 128),
            buffer(UP, 64, 128),
            buffer(UP + 1, 64, 128),
            buffer(UP - 1, 64, 128),
            buffer(15, 16, 128),
            buffer(16, 1024),
            buffer(16, 1024),
            buffer(16, 1024),
            buffer(15, 16, 128),
            buffer(15, 16, 128),
            buffer(64, 1024),
            buffer(16, 1024),
            buffer(64, 1920),
            buffer(64, 2048),
            buffer(64, 1920),
            buffer(15, 64, 128),
            buffer(15, 16, 128),
            buffer(UP, 64, 128),
            buffer(len(ROUNDS) - 1, 64, 128),
            buffer(15, 64, 128),
            buffer(15, 16, 128),
            buffer(30, 64, 128),
            buffer(48, 16, 128),
            buffer(90, 16, 128),
            buffer(len(ROUNDS), 40, 128),
            buffer(MESSAGES, 40, 128),
            pltpu.SemaphoreType.DMA((MESSAGES,)),
            pltpu.SemaphoreType.DMA((MESSAGES,)),
            pltpu.SemaphoreType.DMA((4,)),
            pltpu.SemaphoreType.DMA((4,)),
            pltpu.SemaphoreType.DMA((2 * UP + len(ROUNDS) + 4,)),
        ],
        compiler_params=pltpu.CompilerParams(collective_id=0, has_side_effects=True),
    )(
        near_partner,
        far_partner,
        leaf_basis,
        rhs,
        local_transfer,
        near_blocks,
        local_coupling,
        dev_transfer,
        grp_transfer,
        dev_coupling,
        grp_coupling,
    )


def solution(mesh):
    return jax.shard_map(
        shards,
        mesh=mesh,
        in_specs=(
            P(None, ("grp", "dev")),
            P(None, ("grp", "dev")),
            P(None, ("grp", "dev")),
            P(("grp", "dev")),
            P(None, ("grp", "dev")),
            P(None, ("grp", "dev")),
            P(("grp", "dev"), None),
            P("grp", None, None),
            P("grp", None, None),
            P(),
            P(),
        ),
        out_specs=(P(None, ("grp", "dev")), P()),
        check_vma=False,
    )
```
